32 devices in a mesh: dp: 2 (over y), head: 4 (over x, core), col: 4 (over z).
Axes of the slice: x: 2, y: 2, z: 4, core: 2. Of those that a mesh axis runs over, the one named last changes fastest.
Arguments:
- encoder_token_ids: int32 [8, 1024], P('dp', ('head', 'col')), may hold values from 0 to 32127
- decoder_token_ids: int32 [8, 1024], P('dp', ('head', 'col')), may hold values from 0 to 32127
- target_token_ids: int32 [8, 1024], P('dp', ('head', 'col')), may hold values from 0 to 32127
- target_count_mask: int32 [8, 1024], P('dp', ('head', 'col')), may hold values from 0 to 1, as said below
- encoder_document_length: int32 [8, 4], P('dp'), may hold values from 1 to 512, 1024 in all within a row
- decoder_document_length: int32 [8, 4], P('dp'), may hold values from 1 to 512, 1024 in all within a row
- embedding: bfloat16 [32128, 768], P('col'), may hold values from -6 to 6
- attention_projection_weight: bfloat16 [3, 3, 768, 768], replicated, may hold values from -0.21875 to 0.21875
- attention_output_weight: bfloat16 [3, 768, 768], replicated, may hold values from -1.75 to 1.75
- feedforward_weight: bfloat16 [2, 2, 3072, 768], P(None, None, 'col'), may hold values from -0.21875 to 0.21875
- norm_gain_rows: float32 [7, 768], replicated, may hold values from 0.5 to 1.5
- earlier_down_weight: bfloat16 [6, 14, 8, 768], replicated, may hold values from -0.21875 to 0.21875
- adapter_down_weight: float32 [6, 8, 768], replicated, may hold values from -0.21875 to 0.21875
- adapter_up_weight: float32 [6, 8, 768], replicated, may hold values from -1 to 1
- down_first_moment: float32 [6, 8, 768], replicated, may hold values from -0.0546875 to 0.0546875
- down_second_moment: float32 [6, 8, 768], replicated, may hold values from 1.0986328e-06 to 4.394531e-06
- up_first_moment: float32 [6, 8, 768], replicated, may hold values from -0.015625 to 0.015625
- up_second_moment: float32 [6, 8, 768], replicated, may hold values from 1.2207032e-07 to 4.882813e-07
- optimizer_step_count: int32 [1], replicated, may hold values from 2 to 20
Outputs:
- loss_scalar: float32 [], replicated
- updated_down_weight: float32 [6, 8, 768], replicated
- down_first_updated: float32 [6, 8, 768], replicated
- down_second_updated: float32 [6, 8, 768], replicated
- updated_up_weight: float32 [6, 8, 768], replicated
- up_first_updated: float32 [6, 8, 768], replicated
- up_second_updated: float32 [6, 8, 768], replicated
The draws below stay inside these ranges and needn't reach their ends.
Inputs may be any that keep to these rules, and one draw needn't show every extreme that they name: `encoder_document_length`: the 4 lengths of a row sum to 1024; the longest is 512. `decoder_document_length`: the 4 lengths of a row sum to 1024; the longest is 512. `target_count_mask`: the last position of every row is 1.
All inputs are finite; a program needn't handle non-finite values.
Results may differ from the reference program's by a relative error of at most 0.0027.
The reference program's roundings to bfloat16 on the way count: a program that leaves them out, or rounds other values in their place, can miss the bound.
Values may be sent and summed in bfloat16 or wider, within the bound.
No kernel may reach another device: no remote copies, remote signals or barrier semaphores. Data moves between devices by JAX's collectives and lax.ppermute only.
A program may use at most 192 MiB of HBM per device.

```python
import math
import jax
import jax.numpy as jnp
import numpy as np
from jax import lax

MODEL_DIMENSION = 768
HEADS = 12
HEAD_DIM = 64
FF = 3072
VOCAB = 32128
ADAPTER_RANK = 8
OLD = 14
ADAPTER_COUNT = 6
SEGS = 4
LEN = 1024
MOST = 512
ROWS = 8
TOKENS = 8192


def draw_target_count_mask(key, part):
    rows_i = jnp.arange(ROWS, dtype=jnp.int32)[:, None]
    places = jnp.arange(LEN, dtype=jnp.int32)[None, :]
    thresh = 200 + 700 * (rows_i * (LEN - 1) + places * (ROWS - 1)) // (2 * (ROWS - 1) * (LEN - 1))
    drawn_at = jax.random.randint(key, (ROWS, LEN), 0, 1000)
    return jnp.where((drawn_at < thresh) | (places == LEN - 1), 1, 0).astype(jnp.int32)


def plant(result, key, least, largest):
    longest = result.shape.index(max(result.shape))
    spots = []
    for shift in (0, 1):
        where = [jax.random.randint(jax.random.fold_in(key, axis), (), 0, length) for axis, length in enumerate(result.shape)]
        where[longest] = (where[longest] + shift) % result.shape[longest]
        spots.append(tuple(where))
    return result.at[spots[0]].set(least).at[spots[1]].set(largest)


def block_scale(stream_key, shape, shards, low, top_value):
    factor_of = 1.0
    for dim, parts in shards:
        steps = jax.random.uniform(jax.random.fold_in(jax.random.fold_in(stream_key, 6), dim), (parts,), jnp.float32, low / len(shards), top_value / len(shards))
        factor_of = factor_of * jnp.repeat(jnp.exp(steps), shape[dim] // parts).reshape((-1,) + (1,) * (len(shape) - 1 - dim))
    return factor_of


def rank_bounds(number_of, skew):
    loads = [(1 << 20) // math.isqrt(rank ** skew) + 1 for rank in range(1, number_of + 1)]
    spread = 1 + sum(loads) // (1 << 30)
    return np.cumsum(np.array([max(1, weight // spread) for weight in loads]))


def ranked(key, extent, count, skew):
    grid = rank_bounds(count, skew)
    ticket = jax.random.randint(jax.random.fold_in(key, 1), extent, 0, int(grid[count - 1]))
    grade = jnp.searchsorted(jnp.asarray(grid, jnp.int32), ticket, side="right")
    return jax.random.permutation(jax.random.fold_in(key, 2), count)[grade].astype(jnp.int32)


def profile(amount, total, limit, skew):
    weights = [(1 << 20) // math.isqrt(rank ** skew) + 1 for rank in range(2, amount + 1)]
    rest, given = total - limit - (amount - 1), [1] * (amount - 1)
    while rest > 0:
        free = [i for i in range(amount - 1) if given[i] < limit]
        pool, left = sum([weights[i] for i in free]), rest
        for i in free:
            extra = min(limit - given[i], max(1, left * weights[i] // pool), rest)
            given[i] = given[i] + extra
            rest = rest - extra
    return np.array([limit] + given)


def uneven(stream_key, number_of, total, bound, lean):
    if number_of == 2:
        one = jax.random.randint(stream_key, (), max(1, total - bound), min(bound, total - 1) + 1)
        return jnp.stack([one, total - one])
    sizes = jnp.asarray(profile(number_of, total, bound, lean), jnp.int32)
    pairs = (number_of - 1) // 2
    source_of, sink = sizes[1:1 + 2 * pairs:2], sizes[2:2 + 2 * pairs:2]
    slack = jnp.minimum(source_of - 1, bound - sink)
    shifted = jax.random.randint(jax.random.fold_in(stream_key, 1), (pairs,), 0, 1 << 20) % (slack + 1)
    sizes = sizes.at[1:1 + 2 * pairs:2].set(source_of - shifted).at[2:2 + 2 * pairs:2].set(sink + shifted)
    return sizes[jax.random.permutation(jax.random.fold_in(stream_key, 2), number_of)]


def scatter_about(rng, shape, deviation, limit, cuts=(), kind=jnp.bfloat16):
    entries = deviation * jax.random.normal(rng, shape, jnp.float32)
    if cuts:
        entries = entries * block_scale(rng, shape, cuts, -0.22, 0.18)
    return jnp.clip(entries, -limit, limit).astype(kind)


def setup_inputs(seed: int = 0) -> dict:
    key_list = jax.random.split(jax.random.key(seed), 20)
    return {
        "encoder_token_ids": plant(ranked(key_list[0], (ROWS, LEN), VOCAB, 2), jax.random.fold_in(key_list[0], 3), 0, VOCAB - 1).astype(jnp.int32),
        "decoder_token_ids": plant(ranked(key_list[1], (ROWS, LEN), VOCAB, 2), jax.random.fold_in(key_list[1], 3), 0, VOCAB - 1).astype(jnp.int32),
        "target_token_ids": plant(ranked(key_list[2], (ROWS, LEN), VOCAB, 2), jax.random.fold_in(key_list[2], 3), 0, VOCAB - 1).astype(jnp.int32),
        "target_count_mask": draw_target_count_mask(jax.random.fold_in(key_list[19], 71), 0),
        "encoder_document_length": jax.vmap(lambda own: uneven(own, SEGS, LEN, MOST, 2))(jax.random.split(key_list[4], ROWS)).reshape((ROWS, SEGS)).astype(jnp.int32),
        "decoder_document_length": jax.vmap(lambda own: uneven(own, SEGS, LEN, MOST, 2))(jax.random.split(key_list[5], ROWS)).reshape((ROWS, SEGS)).astype(jnp.int32),
        "embedding": scatter_about(key_list[6], (VOCAB, MODEL_DIMENSION), 1.0, 6.0, ((0, 4),)),
        "attention_projection_weight": scatter_about(key_list[7], (3, 3, MODEL_DIMENSION, MODEL_DIMENSION), MODEL_DIMENSION ** -0.5, 0.21875),
        "attention_output_weight": scatter_about(key_list[8], (3, MODEL_DIMENSION, MODEL_DIMENSION), (MODEL_DIMENSION // 64) ** -0.5, 1.75),
        "feedforward_weight": scatter_about(key_list[9], (2, 2, FF, MODEL_DIMENSION), MODEL_DIMENSION ** -0.5, 0.21875, ((2, 4),)),
        "norm_gain_rows": jnp.clip(1.0 + 0.1 * jax.random.normal(key_list[10], (7, MODEL_DIMENSION), jnp.float32), 0.5, 1.5),
        "earlier_down_weight": scatter_about(key_list[11], (ADAPTER_COUNT, OLD, ADAPTER_RANK, MODEL_DIMENSION), MODEL_DIMENSION ** -0.5, 0.21875),
        "adapter_down_weight": scatter_about(key_list[12], (ADAPTER_COUNT, ADAPTER_RANK, MODEL_DIMENSION), MODEL_DIMENSION ** -0.5, 0.21875, (), jnp.float32),
        "adapter_up_weight": scatter_about(key_list[13], (ADAPTER_COUNT, ADAPTER_RANK, MODEL_DIMENSION), (ADAPTER_RANK * 4) ** -0.5, 1.0, (), jnp.float32),
        "down_first_moment": scatter_about(key_list[14], (ADAPTER_COUNT, ADAPTER_RANK, MODEL_DIMENSION), (0.33 / TOKENS ** 0.5), 0.0546875, (), jnp.float32),
        "down_second_moment": jnp.clip(jnp.exp(jax.random.uniform(key_list[15], (ADAPTER_COUNT, ADAPTER_RANK, MODEL_DIMENSION), jnp.float32, math.log(1.0986327652062755e-06), math.log(4.394531060825102e-06))), 1.0986327652062755e-06, 4.394531060825102e-06),
        "up_first_moment": scatter_about(key_list[16], (ADAPTER_COUNT, ADAPTER_RANK, MODEL_DIMENSION), (0.11 / TOKENS ** 0.5), 0.015625, (), jnp.float32),
        "up_second_moment": jnp.clip(jnp.exp(jax.random.uniform(key_list[17], (ADAPTER_COUNT, ADAPTER_RANK, MODEL_DIMENSION), jnp.float32, math.log(1.2207031829802872e-07), math.log(4.882812731921149e-07))), 1.2207031829802872e-07, 4.882812731921149e-07),
        "optimizer_step_count": jax.random.randint(key_list[18], (1,), 2, 21).astype(jnp.int32),
    }


ADAPTER_SCALE = 2.0
ORTH_WEIGHT = 0.2
BASE_NORM_WEIGHT = 0.02
DOWN_STEP_RATE = 0.05
UP_STEP_RATE = 0.2
BETA_ONE = 0.9
BETA_TWO = 0.999
ADAM_EPS = 1e-08
DECAY = 0.01
NEG_FILL = -1e+30

@jax.custom_vjp
def low(v):
    return lax.optimization_barrier(v.astype(jnp.bfloat16)).astype(jnp.float32)

@jax.custom_vjp
def low_back(v):
    return v

def low_keep(v):
    return (low(v), None)

def low_pass(kept, grad):
    return (grad,)

def back_keep(v):
    return (v, None)

def back_low(kept, grad):
    return (low(grad),)
low.defvjp(low_keep, low_pass)
low_back.defvjp(back_keep, back_low)

def multiplier(left_side, right_side):
    return jnp.dot(left_side, right_side, precision=lax.Precision.HIGHEST)

def rms_norm(values, gain_row):
    return values * lax.rsqrt(lax.optimization_barrier(jnp.mean(values * values, axis=-1, keepdims=True)) + 1e-06) * gain_row

def segment_of(lengths):
    bounds = jnp.cumsum(lengths, dtype=jnp.int32)
    places = jnp.arange(LEN, dtype=jnp.int32)
    return lax.optimization_barrier(jnp.sum((places[:, None] >= bounds[None, :-1]).astype(jnp.int32), axis=1, dtype=jnp.int32))

def attend(queries, key_rows, value_rows, allowed):
    shaped = (LEN, HEADS, HEAD_DIM)
    scores = jnp.einsum('qhd,khd->hqk', queries.reshape(shaped), key_rows.reshape(shaped), precision=lax.Precision.HIGHEST)
    scores = low_back(scores * HEAD_DIM ** (-0.5))
    scores = jnp.where(allowed[None], scores, NEG_FILL)
    row_top = lax.optimization_barrier(jnp.max(scores, axis=2, keepdims=True))
    exponent = jnp.exp(scores - row_top)
    probs = low(exponent / lax.optimization_barrier(jnp.sum(exponent, axis=2, keepdims=True)))
    mixed_heads = jnp.einsum('hqk,khd->qhd', probs, value_rows.reshape(shaped), precision=lax.Precision.HIGHEST)
    return low(low_back(mixed_heads.reshape(LEN, MODEL_DIMENSION)))

def attention(query_in, key_in, qkv_w, out_w, down_low_rank, up_low_rank, slot_at, allowed):

    def adapted(normed_input, base_weight, adapter_selector):
        rank_inner_product = low(low_back(multiplier(normed_input, down_low_rank[adapter_selector].T)))
        return multiplier(normed_input, base_weight) + ADAPTER_SCALE * multiplier(rank_inner_product, up_low_rank[adapter_selector])
    queries = low(low_back(adapted(query_in, qkv_w[0], 2 * slot_at)))
    key_rows = low(low_back(multiplier(key_in, qkv_w[1])))
    value_rows = low(low_back(adapted(key_in, qkv_w[2], 2 * slot_at + 1)))
    mixed_heads = attend(queries, key_rows, value_rows, allowed)
    return low_back(multiplier(mixed_heads, out_w))

def feed_forward(normed_input, ffn_pair):
    pre_act = low_back(multiplier(normed_input, ffn_pair[0].T))
    hidden = low(jnp.maximum(pre_act, 0.0))
    return low_back(multiplier(hidden, ffn_pair[1]))

def adam_update(weights, gradient, first_moment, second_moment, step_rate, step_count_float):
    first_new = BETA_ONE * first_moment + (1.0 - BETA_ONE) * gradient
    second_new = BETA_TWO * second_moment + (1.0 - BETA_TWO) * gradient * gradient
    first_hat = first_new / (1.0 - BETA_ONE ** step_count_float)
    second_hat = second_new / (1.0 - BETA_TWO ** step_count_float)
    weights_new = weights - step_rate * (first_hat / (jnp.sqrt(second_hat) + ADAM_EPS) + DECAY * weights)
    return (weights_new, first_new, second_new)

def reference(encoder_token_ids, decoder_token_ids, target_token_ids, target_count_mask, encoder_document_length, decoder_document_length, embedding, attention_projection_weight, attention_output_weight, feedforward_weight, norm_gain_rows, earlier_down_weight, adapter_down_weight, adapter_up_weight, down_first_moment, down_second_moment, up_first_moment, up_second_moment, optimizer_step_count):
    table_float = embedding.astype(jnp.float32)
    qkv_all = attention_projection_weight.astype(jnp.float32)
    out_all = attention_output_weight.astype(jnp.float32)
    ffn_all = feedforward_weight.astype(jnp.float32)
    earlier_down_float = earlier_down_weight.astype(jnp.float32)
    target_count = jnp.sum(target_count_mask.astype(jnp.float32))
    places = jnp.arange(LEN, dtype=jnp.int32)

    def compute_loss(down_weights, up_weights):
        down_low_rank = low(down_weights)
        up_low_rank = low(up_weights)

        def row_loss(running, row_data):
            enc_row, dec_row, target_row, mask_row, enc_len, dec_len = row_data
            enc_seg = segment_of(enc_len)
            dec_seg = segment_of(dec_len)
            enc_allow = enc_seg[:, None] == enc_seg[None, :]
            dec_allow = (dec_seg[:, None] == dec_seg[None, :]) & (places[None, :] <= places[:, None])
            cross_allow = dec_seg[:, None] == enc_seg[None, :]
            hidden = table_float[enc_row]
            normed_input = low(rms_norm(hidden, norm_gain_rows[0]))
            hidden = hidden + attention(normed_input, normed_input, qkv_all[0], out_all[0], down_low_rank, up_low_rank, 0, enc_allow)
            hidden = hidden + feed_forward(low(rms_norm(hidden, norm_gain_rows[1])), ffn_all[0])
            encoded = low(rms_norm(hidden, norm_gain_rows[2]))
            dec_state = table_float[dec_row]
            normed_input = low(rms_norm(dec_state, norm_gain_rows[3]))
            dec_state = dec_state + attention(normed_input, normed_input, qkv_all[1], out_all[1], down_low_rank, up_low_rank, 1, dec_allow)
            dec_state = dec_state + attention(low(rms_norm(dec_state, norm_gain_rows[4])), encoded, qkv_all[2], out_all[2], down_low_rank, up_low_rank, 2, cross_allow)
            dec_state = dec_state + feed_forward(low(rms_norm(dec_state, norm_gain_rows[5])), ffn_all[1])
            final_rows = low(rms_norm(dec_state, norm_gain_rows[6]) * MODEL_DIMENSION ** (-0.5))
            logits = low_back(multiplier(final_rows, table_float.T))
            row_top = lax.optimization_barrier(jnp.max(logits, axis=1, keepdims=True))
            log_total = row_top[:, 0] + jnp.log(lax.optimization_barrier(jnp.sum(jnp.exp(logits - row_top), axis=1)))
            picked = jnp.take_along_axis(logits, target_row[:, None], axis=1)[:, 0]
            return (running + jnp.sum(mask_row.astype(jnp.float32) * (log_total - picked)), None)
        ce_total, unused = lax.scan(jax.checkpoint(row_loss), jnp.zeros((), jnp.float32), (encoder_token_ids, decoder_token_ids, target_token_ids, target_count_mask, encoder_document_length, decoder_document_length))
        intersection = jnp.einsum('hygm,hvm->hygv', earlier_down_float, down_weights, precision=lax.Precision.HIGHEST)
        return ce_total / target_count + ORTH_WEIGHT * jnp.sum(intersection * intersection) + BASE_NORM_WEIGHT * jnp.sum(up_weights * up_weights)
    loss_scalar, backward_function = jax.vjp(compute_loss, adapter_down_weight, adapter_up_weight)
    down_gradient, up_gradient = backward_function(jnp.ones((), jnp.float32))
    step_count_float = optimizer_step_count[0].astype(jnp.float32)
    updated_down_weight, down_first_updated, down_second_updated = adam_update(adapter_down_weight, down_gradient, down_first_moment, down_second_moment, DOWN_STEP_RATE, step_count_float)
    updated_up_weight, up_first_updated, up_second_updated = adam_update(adapter_up_weight, up_gradient, up_first_moment, up_second_moment, UP_STEP_RATE, step_count_float)
    return (loss_scalar, updated_down_weight, down_first_updated, down_second_updated, updated_up_weight, up_first_updated, up_second_updated)
```

```python
import jax
import jax.numpy as jnp
from jax import lax
from jax.sharding import PartitionSpec as P

MODEL_DIMENSION = 768
HEAD_DIM = 64
ADAPTER_RANK = 8
LEN = 1024


ADAPTER_SCALE = 2.0
ORTH_WEIGHT = 0.2
BASE_NORM_WEIGHT = 0.02
DOWN_STEP_RATE = 0.05
UP_STEP_RATE = 0.2
BETA_ONE = 0.9
BETA_TWO = 0.999
ADAM_EPS = 1e-08
DECAY = 0.01
NEG_FILL = -1e30


def swapped(x, axis, step):
    return lax.ppermute(x, axis, [(i, i ^ step) for i in range(lax.axis_size(axis))])


def summed(x, axes):
    for axis in axes:
        step = 1
        while step < lax.axis_size(axis):
            x = jax.tree.map(lambda part: part + swapped(part, axis, step), x)
            step *= 2
    return x


def collected(x, axis):
    n = lax.axis_size(axis)
    me = lax.axis_index(axis)
    parts = jnp.stack([x] + [swapped(x, axis, step) for step in range(1, n)])
    return jnp.stack(
        [lax.dynamic_index_in_dim(parts, me ^ at, 0, keepdims=False) for at in range(n)]
    )


def scattered_sum(x, axis):
    n = lax.axis_size(axis)
    me = lax.axis_index(axis)
    total = lax.dynamic_index_in_dim(x, me, 0, keepdims=False)
    for step in range(1, n):
        block = lax.dynamic_index_in_dim(x, me ^ step, 0, keepdims=False)
        total = total + swapped(block, axis, step)
    return total


def rms_norm(values, gain_row):
    return values * lax.rsqrt(jnp.mean(values * values, axis=-1, keepdims=True) + 1e-06) * gain_row


def norm_back(values, gain_row, grad_out, scale_by):
    primal, backward_function = jax.vjp(
        lambda inner_vals: rms_norm(inner_vals, gain_row) * scale_by, values
    )
    return backward_function(grad_out)[0]


def segment_of(lengths, length_total):
    bounds = jnp.cumsum(lengths, dtype=jnp.int32)
    places = jnp.arange(length_total, dtype=jnp.int32)
    return jnp.sum(
        (places[:, None] >= bounds[None, :-1]).astype(jnp.int32), axis=1, dtype=jnp.int32
    )


def col_rows(rows_low):
    return lax.all_gather(rows_low, "col", axis=0, tiled=True)


def col_sums(terms):
    return lax.psum_scatter(terms, "col", scatter_dimension=0, tiled=True)


def head_trade(blocks):
    return lax.all_to_all(blocks, "head", split_axis=0, concat_axis=0, tiled=True)


def score_block(q_block, key_rows, seg_block, seg_key, start_at, causal):
    scores = jnp.einsum(
        "qhd,khd->hqk", q_block, key_rows, preferred_element_type=jnp.float32
    ) * HEAD_DIM ** (-0.5)
    allowed = seg_block[:, None] == seg_key[None, :]
    if causal:
        query_at = start_at + jnp.arange(q_block.shape[0], dtype=jnp.int32)
        key_at = jnp.arange(seg_key.shape[0], dtype=jnp.int32)
        allowed = allowed & (key_at[None, :] <= query_at[:, None])
    return jnp.where(allowed[None], scores, NEG_FILL)


def attend_forward(queries, key_rows, value_rows, seg_query, seg_key, causal):
    length_q, heads_here, head_width = queries.shape
    block_rows = min(512, length_q)
    blocks = length_q // block_rows

    def one_block(members):
        q_block, seg_block, start_at = members
        scores = score_block(q_block, key_rows, seg_block, seg_key, start_at, causal)
        row_top = jnp.max(scores, axis=2, keepdims=True)
        exponent = jnp.exp(scores - row_top)
        row_total = jnp.sum(exponent, axis=2, keepdims=True)
        probs_low = (exponent / row_total).astype(jnp.bfloat16)
        mixed_heads = jnp.einsum(
            "hqk,khd->qhd", probs_low, value_rows, preferred_element_type=jnp.float32
        )
        return (mixed_heads.astype(jnp.bfloat16), row_top, row_total)

    starts = jnp.arange(blocks, dtype=jnp.int32) * block_rows
    mixed_heads, row_tops, row_sums = lax.map(
        one_block,
        (
            queries.reshape(blocks, block_rows, heads_here, head_width),
            seg_query.reshape(blocks, block_rows),
            starts,
        ),
    )
    return (mixed_heads.reshape(length_q, heads_here, head_width), row_tops, row_sums)


def attend_backward(
    queries, key_rows, value_rows, seg_query, seg_key, causal, row_tops, row_sums, grad_mixed, want_keys
):
    length_q, heads_here, head_width = queries.shape
    block_rows = min(512, length_q)
    blocks = length_q // block_rows
    score_scale = HEAD_DIM ** (-0.5)

    def one_block(carried, members):
        grad_keys, grad_values = carried
        q_block, seg_block, start_at, top_block, total_block, grad_block = members
        scores = score_block(q_block, key_rows, seg_block, seg_key, start_at, causal)
        probs_f = jnp.exp(scores - top_block) / total_block
        grad_probs = jnp.einsum(
            "qhd,khd->hqk", grad_block, value_rows, preferred_element_type=jnp.float32
        )
        inner_sum = jnp.sum(grad_probs * probs_f, axis=2, keepdims=True)
        grad_scores = (probs_f * (grad_probs - inner_sum)).astype(jnp.bfloat16)
        grad_q = (
            jnp.einsum("hqk,khd->qhd", grad_scores, key_rows, preferred_element_type=jnp.float32)
            * score_scale
        )
        if want_keys:
            grad_keys = (
                grad_keys
                + jnp.einsum(
                    "hqk,qhd->khd", grad_scores, q_block, preferred_element_type=jnp.float32
                )
                * score_scale
            )
        grad_values = grad_values + jnp.einsum(
            "hqk,qhd->khd",
            probs_f.astype(jnp.bfloat16),
            grad_block,
            preferred_element_type=jnp.float32,
        )
        return ((grad_keys, grad_values), grad_q)

    empty_kv = jnp.zeros(key_rows.shape, jnp.float32)
    starts = jnp.arange(blocks, dtype=jnp.int32) * block_rows
    members = (
        queries.reshape(blocks, block_rows, heads_here, head_width),
        seg_query.reshape(blocks, block_rows),
        starts,
        row_tops,
        row_sums,
        grad_mixed.reshape(blocks, block_rows, heads_here, head_width),
    )
    (grad_keys, grad_values), grad_q = lax.scan(one_block, (empty_kv, empty_kv), members)
    return (grad_q.reshape(length_q, heads_here, head_width), grad_keys, grad_values)


def contract(left, right, left_dim, right_dim):
    return lax.dot_general(
        left, right, (((left_dim,), (right_dim,)), ((), ())), preferred_element_type=jnp.float32
    )


def adapter_forward(normed_input, down_one, up_one):
    inner_low = contract(normed_input, down_one, 1, 1).astype(jnp.bfloat16)
    return (inner_low, ADAPTER_SCALE * contract(inner_low, up_one, 1, 0))


def adapter_back(grad_side, inner_low, normed_input, down_one, up_one):
    up_gradient = ADAPTER_SCALE * contract(inner_low, grad_side, 0, 0)
    grad_inner = (ADAPTER_SCALE * contract(grad_side, up_one, 1, 1)).astype(jnp.bfloat16)
    down_gradient = contract(grad_inner, normed_input, 0, 0)
    return (down_gradient, up_gradient, contract(grad_inner, down_one, 1, 0))


def by_head(rows, n_head):
    length, width = rows.shape
    return rows.reshape(length, n_head, width // n_head).transpose(1, 0, 2)


def from_head(blocks):
    n_head, length, width = blocks.shape
    return blocks.transpose(1, 0, 2).reshape(length, n_head * width)


def attention_forward(
    normed_q, normed_kv, qkv_w, out_w, down_pair, up_pair, seg_query, seg_key, causal
):
    n_head = lax.axis_size("head")
    piece_n, model_width = normed_q.shape
    heads_here = model_width // n_head // HEAD_DIM
    inner_q, lifted_q = adapter_forward(normed_q, down_pair[0], up_pair[0])
    inner_v, lifted_v = adapter_forward(normed_kv, down_pair[1], up_pair[1])
    queries = (contract(normed_q, qkv_w[0], 1, 0) + lifted_q).astype(jnp.bfloat16)
    keys = contract(normed_kv, qkv_w[1], 1, 0).astype(jnp.bfloat16)
    values = (contract(normed_kv, qkv_w[2], 1, 0) + lifted_v).astype(jnp.bfloat16)
    got = head_trade(
        jnp.stack([by_head(queries, n_head), by_head(keys, n_head), by_head(values, n_head)], 1)
    )
    queries_a, keys_a, values_a = [
        got[:, kind].reshape(n_head * piece_n, heads_here, HEAD_DIM) for kind in range(3)
    ]
    mixed_heads, row_tops, row_sums = attend_forward(
        queries_a, keys_a, values_a, seg_query, seg_key, causal
    )
    back_rows = from_head(head_trade(mixed_heads.reshape(n_head, piece_n, -1)))
    result = contract(back_rows, out_w, 1, 0)
    return (result, (inner_q, inner_v, queries_a, keys_a, values_a, row_tops, row_sums))


def attention_backward(
    grad_res,
    normed_q,
    normed_kv,
    kept_fwd,
    qkv_w,
    out_w,
    down_pair,
    up_pair,
    seg_query,
    seg_key,
    causal,
    want_inputs,
):
    inner_q, inner_v, queries_a, keys_a, values_a, row_tops, row_sums = kept_fwd
    n_head = lax.axis_size("head")
    head_at = lax.axis_index("head")
    piece_n, model_width = normed_q.shape
    group_w = model_width // n_head
    heads_here = group_w // HEAD_DIM
    grad_back = contract(grad_res.astype(jnp.bfloat16), out_w, 1, 1).astype(jnp.bfloat16)
    grad_mixed = head_trade(by_head(grad_back, n_head))
    grad_q, grad_k, grad_v = attend_backward(
        queries_a,
        keys_a,
        values_a,
        seg_query,
        seg_key,
        causal,
        row_tops,
        row_sums,
        grad_mixed.reshape(n_head * piece_n, heads_here, HEAD_DIM),
        want_inputs,
    )
    grad_q, grad_k, grad_v = [
        part.astype(jnp.bfloat16).reshape(n_head * piece_n, group_w)
        for part in (grad_q, grad_k, grad_v)
    ]
    if not want_inputs:
        inner_both = jnp.concatenate([inner_q, inner_v], axis=1).T
        inner_all = collected(inner_both, "head").transpose(1, 0, 2).reshape(
            2 * ADAPTER_RANK, n_head * piece_n
        )
        partial_inner = []
        up_gradients = []
        for at, grad_side in enumerate((grad_q, grad_v)):
            up_here = lax.dynamic_slice_in_dim(up_pair[at], head_at * group_w, group_w, 1)
            partial_inner.append(contract(up_here, grad_side, 1, 1))
            up_gradients.append(
                lax.dynamic_update_slice_in_dim(
                    jnp.zeros((ADAPTER_RANK, model_width), jnp.float32),
                    ADAPTER_SCALE
                    * contract(
                        inner_all[at * ADAPTER_RANK : (at + 1) * ADAPTER_RANK], grad_side, 1, 0
                    ),
                    head_at * group_w,
                    1,
                )
            )
        partial_inner = jnp.concatenate(partial_inner, axis=0)
        own_inner = scattered_sum(
            partial_inner.reshape(2 * ADAPTER_RANK, n_head, piece_n).transpose(1, 0, 2), "head"
        )
        own_inner = (ADAPTER_SCALE * own_inner).astype(jnp.bfloat16)
        return (
            None,
            None,
            (
                contract(own_inner[:ADAPTER_RANK], normed_q, 1, 0),
                contract(own_inner[ADAPTER_RANK:], normed_kv, 1, 0),
            ),
            tuple(up_gradients),
        )
    got = head_trade(
        jnp.stack([part.reshape(n_head, piece_n, group_w) for part in (grad_q, grad_k, grad_v)], 1)
    )
    grad_qt, grad_kt, grad_vt = [from_head(got[:, kind]) for kind in range(3)]
    down_query, up_query, side_q = adapter_back(
        grad_qt, inner_q, normed_q, down_pair[0], up_pair[0]
    )
    down_value, up_value, side_v = adapter_back(
        grad_vt, inner_v, normed_kv, down_pair[1], up_pair[1]
    )
    normed_query_gradient = contract(grad_qt, qkv_w[0], 1, 1) + side_q
    normed_key_value_gradient = (
        contract(grad_kt, qkv_w[1], 1, 1) + contract(grad_vt, qkv_w[2], 1, 1) + side_v
    )
    return (
        normed_query_gradient,
        normed_key_value_gradient,
        (down_query, down_value),
        (up_query, up_value),
    )


def whole_ffn(weight_pair):
    copies = lax.axis_size("dp") * lax.axis_size("head")
    copy_at = lax.axis_index("dp") * lax.axis_size("head") + lax.axis_index("head")
    units = weight_pair.shape[1] // copies
    share = lax.dynamic_slice_in_dim(weight_pair, copy_at * units, units, 1)
    share = jnp.concatenate([share[0], share[1]], axis=1)
    return lax.all_gather(share, ("dp", "head", "col"), axis=0, tiled=True)


def ffn_forward(normed_input, units):
    model_width = normed_input.shape[-1]
    pre_act = contract(normed_input, units[:, :model_width], 1, 1)
    hidden = jnp.maximum(pre_act, 0.0).astype(jnp.bfloat16)
    return (contract(hidden, units[:, model_width:], 1, 0), pre_act > 0.0)


def ffn_backward(grad_res, active, units):
    model_width = grad_res.shape[-1]
    grad_hidden = contract(grad_res.astype(jnp.bfloat16), units[:, model_width:], 1, 1)
    grad_pre = jnp.where(active, grad_hidden, 0.0).astype(jnp.bfloat16)
    return contract(grad_pre, units[:, :model_width], 1, 0)


def vocab_stats(head_rows, clipped, inside, embedding, n_col):
    model_width = head_rows.shape[1]

    def one_block(members):
        rows_blk, clip_blk, inside_blk = members
        logits = lax.dot_general(
            rows_blk, embedding, (((1,), (1,)), ((), ())), preferred_element_type=jnp.float32
        )
        row_top = jnp.max(logits, axis=1)
        row_total = jnp.sum(jnp.exp(logits - row_top[:, None]), axis=1)
        picked = jnp.take_along_axis(logits, clip_blk[:, None], axis=1)[:, 0]
        return (row_top, row_total, jnp.where(inside_blk, picked, 0.0))

    block_outs = lax.map(
        one_block,
        (
            head_rows.reshape(n_col, -1, model_width),
            clipped.reshape(n_col, -1),
            inside.reshape(n_col, -1),
        ),
    )
    return tuple((member.reshape(-1) for member in block_outs))


def vocab_back(head_rows, clipped, inside, embedding, n_col, log_total, coef_rows):
    model_width = head_rows.shape[1]
    vocab_part = embedding.shape[0]

    def one_block(members):
        rows_blk, clip_blk, inside_blk, total_blk, coef_blk = members
        logits = lax.dot_general(
            rows_blk, embedding, (((1,), (1,)), ((), ())), preferred_element_type=jnp.float32
        )
        probs_f = jnp.exp(logits - total_blk[:, None])
        hits = (jnp.arange(vocab_part, dtype=jnp.int32)[None, :] == clip_blk[:, None]) & inside_blk[
            :, None
        ]
        grad_logits = (coef_blk[:, None] * (probs_f - hits.astype(jnp.float32))).astype(
            jnp.bfloat16
        )
        return jnp.dot(grad_logits, embedding, preferred_element_type=jnp.float32)

    members = (
        head_rows.reshape(n_col, -1, model_width),
        clipped.reshape(n_col, -1),
        inside.reshape(n_col, -1),
        log_total.reshape(n_col, -1),
        coef_rows.reshape(n_col, -1),
    )
    return lax.map(one_block, members).reshape(-1, model_width)


def merge_stats(left_side, right_side):
    top_both = jnp.maximum(left_side[0], right_side[0])
    summed = left_side[1] * jnp.exp(left_side[0] - top_both) + right_side[1] * jnp.exp(
        right_side[0] - top_both
    )
    return (top_both, summed, left_side[2] + right_side[2])


def adam_update(weights, gradient, first_moment, second_moment, step_rate, step_count_float):
    first_new = BETA_ONE * first_moment + (1.0 - BETA_ONE) * gradient
    second_new = BETA_TWO * second_moment + (1.0 - BETA_TWO) * gradient * gradient
    first_hat = first_new / (1.0 - BETA_ONE**step_count_float)
    second_hat = second_new / (1.0 - BETA_TWO**step_count_float)
    weights_new = weights - step_rate * (
        first_hat / (jnp.sqrt(second_hat) + ADAM_EPS) + DECAY * weights
    )
    return (weights_new, first_new, second_new)


def per_device(
    encoder_token_ids,
    decoder_token_ids,
    target_token_ids,
    target_count_mask,
    encoder_document_length,
    decoder_document_length,
    embedding,
    attention_projection_weight,
    attention_output_weight,
    feedforward_weight,
    norm_gain_rows,
    earlier_down_weight,
    adapter_down_weight,
    adapter_up_weight,
    down_first_moment,
    down_second_moment,
    up_first_moment,
    up_second_moment,
    optimizer_step_count,
):
    n_col = lax.axis_size("col")
    col_at = lax.axis_index("col")
    vocab_part, model_width = embedding.shape
    tables = jnp.stack(
        [encoder_token_ids, decoder_token_ids, target_token_ids, target_count_mask]
    )
    tables = collected(tables, "col").transpose(1, 2, 0, 3)
    enc_all, dec_all, target_all, mask_all = tables.reshape(4, -1)

    def lookup(ids_flat):
        local_ids = ids_flat - col_at * vocab_part
        inside_ids = (local_ids >= 0) & (local_ids < vocab_part)
        picked = jnp.take(embedding, jnp.clip(local_ids, 0, vocab_part - 1), axis=0)
        return col_sums(
            jnp.where(inside_ids[:, None], picked, jnp.zeros((), picked.dtype))
        ).astype(jnp.float32)

    enc_state = lookup(enc_all)
    units_enc = whole_ffn(feedforward_weight[0])
    dec_state = lookup(dec_all)
    units_dec = whole_ffn(feedforward_weight[1])
    mask_float = mask_all.astype(jnp.float32)
    target_count = summed(jnp.sum(mask_float), ("dp", "head"))
    down_low_rank = adapter_down_weight.astype(jnp.bfloat16)
    up_low_rank = adapter_up_weight.astype(jnp.bfloat16)
    enc_seg = segment_of(
        lax.dynamic_index_in_dim(encoder_document_length, col_at, 0, keepdims=False), LEN
    )
    dec_seg = segment_of(
        lax.dynamic_index_in_dim(decoder_document_length, col_at, 0, keepdims=False), LEN
    )

    def weights_of(slot_at):
        return (
            attention_projection_weight[slot_at],
            attention_output_weight[slot_at],
            down_low_rank[2 * slot_at : 2 * slot_at + 2],
            up_low_rank[2 * slot_at : 2 * slot_at + 2],
        )

    enc_normed = rms_norm(enc_state, norm_gain_rows[0]).astype(jnp.bfloat16)
    branch_out, kept_enc = attention_forward(
        enc_normed, enc_normed, *weights_of(0), enc_seg, enc_seg, False
    )
    enc_mid = enc_state + branch_out
    dec_normed = rms_norm(dec_state, norm_gain_rows[3]).astype(jnp.bfloat16)
    branch_out, kept_self = attention_forward(
        dec_normed, dec_normed, *weights_of(1), dec_seg, dec_seg, True
    )
    dec_one = dec_state + branch_out
    branch_out, active_enc = ffn_forward(
        rms_norm(enc_mid, norm_gain_rows[1]).astype(jnp.bfloat16), units_enc
    )
    enc_last = enc_mid + branch_out
    encoded = rms_norm(enc_last, norm_gain_rows[2]).astype(jnp.bfloat16)
    cross_normed = rms_norm(dec_one, norm_gain_rows[4]).astype(jnp.bfloat16)
    branch_out, kept_cross = attention_forward(
        cross_normed, encoded, *weights_of(2), dec_seg, enc_seg, False
    )
    dec_two = dec_one + branch_out
    branch_out, active_dec = ffn_forward(
        rms_norm(dec_two, norm_gain_rows[5]).astype(jnp.bfloat16), units_dec
    )
    dec_three = dec_two + branch_out
    head_scale = MODEL_DIMENSION ** (-0.5)
    final_rows = (rms_norm(dec_three, norm_gain_rows[6]) * head_scale).astype(jnp.bfloat16)
    head_rows = col_rows(final_rows)
    local_t = target_all - col_at * vocab_part
    inside = (local_t >= 0) & (local_t < vocab_part)
    clipped = jnp.clip(local_t, 0, vocab_part - 1)
    stats = vocab_stats(head_rows, clipped, inside, embedding, n_col)
    step = 1
    while step < n_col:
        others = swapped(jnp.stack(stats), "col", step)
        stats = merge_stats(stats, (others[0], others[1], others[2]))
        step *= 2
    row_top, row_total, row_target = stats
    log_total = row_top + jnp.log(row_total)
    ce_local = jnp.sum(mask_float * (log_total - row_target))
    ce_total = summed(ce_local, ("dp", "head"))
    grad_rows = vocab_back(
        head_rows, clipped, inside, embedding, n_col, log_total, mask_float / target_count
    )
    grad_final = col_sums(grad_rows)
    grad_dec = norm_back(dec_three, norm_gain_rows[6], grad_final, head_scale)
    grad_dec = grad_dec + norm_back(
        dec_two, norm_gain_rows[5], ffn_backward(grad_dec, active_dec, units_dec), 1.0
    )
    normed_query_gradient, grad_encoded, downs_cross, ups_cross = attention_backward(
        grad_dec, cross_normed, encoded, kept_cross, *weights_of(2), dec_seg, enc_seg, False, True
    )
    cross_sums = summed(jnp.stack(downs_cross + ups_cross), ("head", "dp", "col"))
    grad_dec = grad_dec + norm_back(dec_one, norm_gain_rows[4], normed_query_gradient, 1.0)
    unused_q, unused_kv, downs_self, ups_self = attention_backward(
        grad_dec, dec_normed, dec_normed, kept_self, *weights_of(1), dec_seg, dec_seg, True, False
    )
    grad_enc = norm_back(enc_last, norm_gain_rows[2], grad_encoded, 1.0)
    grad_enc = grad_enc + norm_back(
        enc_mid, norm_gain_rows[1], ffn_backward(grad_enc, active_enc, units_enc), 1.0
    )
    unused_q, unused_kv, downs_enc, ups_enc = attention_backward(
        grad_enc, enc_normed, enc_normed, kept_enc, *weights_of(0), enc_seg, enc_seg, False, False
    )
    self_sums = summed(
        jnp.stack(downs_enc + downs_self + ups_enc + ups_self), ("head", "dp", "col")
    )
    down_penalty_sum = jnp.concatenate([self_sums[:4], cross_sums[:2]])
    up_penalty_sum = jnp.concatenate([self_sums[4:], cross_sums[2:]])
    earlier_down_float = earlier_down_weight.astype(jnp.float32)
    intersection = jnp.einsum(
        "hygm,hvm->hygv", earlier_down_float, adapter_down_weight, precision=lax.Precision.HIGHEST
    )
    penalty = ORTH_WEIGHT * jnp.sum(intersection * intersection) + BASE_NORM_WEIGHT * jnp.sum(
        adapter_up_weight * adapter_up_weight
    )
    down_penalty_sum = down_penalty_sum + 2.0 * ORTH_WEIGHT * jnp.einsum(
        "aoij,aoid->ajd", intersection, earlier_down_float, precision=lax.Precision.HIGHEST
    )
    up_penalty_sum = up_penalty_sum + 2.0 * BASE_NORM_WEIGHT * adapter_up_weight
    loss_scalar = ce_total / target_count + penalty
    step_count_float = optimizer_step_count[0].astype(jnp.float32)
    updated_down_weight, down_first_updated, down_second_updated = adam_update(
        adapter_down_weight,
        down_penalty_sum,
        down_first_moment,
        down_second_moment,
        DOWN_STEP_RATE,
        step_count_float,
    )
    updated_up_weight, up_first_updated, up_second_updated = adam_update(
        adapter_up_weight,
        up_penalty_sum,
        up_first_moment,
        up_second_moment,
        UP_STEP_RATE,
        step_count_float,
    )
    return (
        loss_scalar,
        updated_down_weight,
        down_first_updated,
        down_second_updated,
        updated_up_weight,
        up_first_updated,
        up_second_updated,
    )


def solution(mesh):
    in_specs = (
        P("dp", ("head", "col")),
        P("dp", ("head", "col")),
        P("dp", ("head", "col")),
        P("dp", ("head", "col")),
        P("dp", None),
        P("dp", None),
        P("col", None),
        P(),
        P(),
        P(None, None, "col", None),
        P(),
        P(),
        P(),
        P(),
        P(),
        P(),
        P(),
        P(),
        P(),
    )
    out_specs = (P(), P(), P(), P(), P(), P(), P())
    return jax.shard_map(
        per_device, mesh=mesh, in_specs=in_specs, out_specs=out_specs, check_vma=False
    )
```

```python
import functools

import jax
import jax.numpy as jnp
from jax import lax
from jax.experimental import pallas as pl
from jax.experimental.pallas import tpu as pltpu
from jax.sharding import PartitionSpec as P

MODEL_DIMENSION = 768
HEAD_DIM = 64
ADAPTER_RANK = 8
LEN = 1024


ADAPTER_SCALE = 2.0
ORTH_WEIGHT = 0.2
BASE_NORM_WEIGHT = 0.02
DOWN_STEP_RATE = 0.05
UP_STEP_RATE = 0.2
BETA_ONE = 0.9
BETA_TWO = 0.999
ADAM_EPS = 1e-08
DECAY = 0.01
NEG_FILL = -1e30


def swapped(x, axis, step):
    return lax.ppermute(x, axis, [(i, i ^ step) for i in range(lax.axis_size(axis))])


def summed(x, axes):
    for axis in axes:
        step = 1
        while step < lax.axis_size(axis):
            x = jax.tree.map(lambda part: part + swapped(part, axis, step), x)
            step *= 2
    return x


def collected(x, axis):
    n = lax.axis_size(axis)
    me = lax.axis_index(axis)
    parts = jnp.stack([x] + [swapped(x, axis, step) for step in range(1, n)])
    return jnp.stack(
        [lax.dynamic_index_in_dim(parts, me ^ at, 0, keepdims=False) for at in range(n)]
    )


def scattered_sum(x, axis):
    n = lax.axis_size(axis)
    me = lax.axis_index(axis)
    total = lax.dynamic_index_in_dim(x, me, 0, keepdims=False)
    for step in range(1, n):
        block = lax.dynamic_index_in_dim(x, me ^ step, 0, keepdims=False)
        total = total + swapped(block, axis, step)
    return total


def rms_norm(values, gain_row):
    return values * lax.rsqrt(jnp.mean(values * values, axis=-1, keepdims=True) + 1e-06) * gain_row


def norm_back(values, gain_row, grad_out, scale_by):
    primal, backward_function = jax.vjp(
        lambda inner_vals: rms_norm(inner_vals, gain_row) * scale_by, values
    )
    return backward_function(grad_out)[0]


def segment_of(lengths, length_total):
    bounds = jnp.cumsum(lengths, dtype=jnp.int32)
    places = jnp.arange(length_total, dtype=jnp.int32)
    return jnp.sum(
        (places[:, None] >= bounds[None, :-1]).astype(jnp.int32), axis=1, dtype=jnp.int32
    )


def col_rows(rows_low):
    return lax.all_gather(rows_low, "col", axis=0, tiled=True)


def col_sums(terms):
    return lax.psum_scatter(terms, "col", scatter_dimension=0, tiled=True)


def head_trade(blocks):
    return lax.all_to_all(blocks, "head", split_axis=0, concat_axis=0, tiled=True)


def score_block(q_block, key_rows, seg_block, seg_key, start_at, causal):
    scores = jnp.einsum(
        "qhd,khd->hqk", q_block, key_rows, preferred_element_type=jnp.float32
    ) * HEAD_DIM ** (-0.5)
    allowed = seg_block[:, None] == seg_key[None, :]
    if causal:
        query_at = start_at + jnp.arange(q_block.shape[0], dtype=jnp.int32)
        key_at = jnp.arange(seg_key.shape[0], dtype=jnp.int32)
        allowed = allowed & (key_at[None, :] <= query_at[:, None])
    return jnp.where(allowed[None], scores, NEG_FILL)


def attend_forward(queries, key_rows, value_rows, seg_query, seg_key, causal):
    length_q, heads_here, head_width = queries.shape
    block_rows = min(512, length_q)
    blocks = length_q // block_rows

    def one_block(members):
        q_block, seg_block, start_at = members
        scores = score_block(q_block, key_rows, seg_block, seg_key, start_at, causal)
        row_top = jnp.max(scores, axis=2, keepdims=True)
        exponent = jnp.exp(scores - row_top)
        row_total = jnp.sum(exponent, axis=2, keepdims=True)
        probs_low = (exponent / row_total).astype(jnp.bfloat16)
        mixed_heads = jnp.einsum(
            "hqk,khd->qhd", probs_low, value_rows, preferred_element_type=jnp.float32
        )
        return (mixed_heads.astype(jnp.bfloat16), row_top, row_total)

    starts = jnp.arange(blocks, dtype=jnp.int32) * block_rows
    mixed_heads, row_tops, row_sums = lax.map(
        one_block,
        (
            queries.reshape(blocks, block_rows, heads_here, head_width),
            seg_query.reshape(blocks, block_rows),
            starts,
        ),
    )
    return (mixed_heads.reshape(length_q, heads_here, head_width), row_tops, row_sums)


def attend_backward(
    queries, key_rows, value_rows, seg_query, seg_key, causal, row_tops, row_sums, grad_mixed, want_keys
):
    length_q, heads_here, head_width = queries.shape
    block_rows = min(512, length_q)
    blocks = length_q // block_rows
    score_scale = HEAD_DIM ** (-0.5)

    def one_block(carried, members):
        grad_keys, grad_values = carried
        q_block, seg_block, start_at, top_block, total_block, grad_block = members
        scores = score_block(q_block, key_rows, seg_block, seg_key, start_at, causal)
        probs_f = jnp.exp(scores - top_block) / total_block
        grad_probs = jnp.einsum(
            "qhd,khd->hqk", grad_block, value_rows, preferred_element_type=jnp.float32
        )
        inner_sum = jnp.sum(grad_probs * probs_f, axis=2, keepdims=True)
        grad_scores = (probs_f * (grad_probs - inner_sum)).astype(jnp.bfloat16)
        grad_q = (
            jnp.einsum("hqk,khd->qhd", grad_scores, key_rows, preferred_element_type=jnp.float32)
            * score_scale
        )
        if want_keys:
            grad_keys = (
                grad_keys
                + jnp.einsum(
                    "hqk,qhd->khd", grad_scores, q_block, preferred_element_type=jnp.float32
                )
                * score_scale
            )
        grad_values = grad_values + jnp.einsum(
            "hqk,qhd->khd",
            probs_f.astype(jnp.bfloat16),
            grad_block,
            preferred_element_type=jnp.float32,
        )
        return ((grad_keys, grad_values), grad_q)

    empty_kv = jnp.zeros(key_rows.shape, jnp.float32)
    starts = jnp.arange(blocks, dtype=jnp.int32) * block_rows
    members = (
        queries.reshape(blocks, block_rows, heads_here, head_width),
        seg_query.reshape(blocks, block_rows),
        starts,
        row_tops,
        row_sums,
        grad_mixed.reshape(blocks, block_rows, heads_here, head_width),
    )
    (grad_keys, grad_values), grad_q = lax.scan(one_block, (empty_kv, empty_kv), members)
    return (grad_q.reshape(length_q, heads_here, head_width), grad_keys, grad_values)


def contract(left, right, left_dim, right_dim):
    return lax.dot_general(
        left, right, (((left_dim,), (right_dim,)), ((), ())), preferred_element_type=jnp.float32
    )


def adapter_forward(normed_input, down_one, up_one):
    inner_low = contract(normed_input, down_one, 1, 1).astype(jnp.bfloat16)
    return (inner_low, ADAPTER_SCALE * contract(inner_low, up_one, 1, 0))


def adapter_back(grad_side, inner_low, normed_input, down_one, up_one):
    up_gradient = ADAPTER_SCALE * contract(inner_low, grad_side, 0, 0)
    grad_inner = (ADAPTER_SCALE * contract(grad_side, up_one, 1, 1)).astype(jnp.bfloat16)
    down_gradient = contract(grad_inner, normed_input, 0, 0)
    return (down_gradient, up_gradient, contract(grad_inner, down_one, 1, 0))


def by_head(rows, n_head):
    length, width = rows.shape
    return rows.reshape(length, n_head, width // n_head).transpose(1, 0, 2)


def from_head(blocks):
    n_head, length, width = blocks.shape
    return blocks.transpose(1, 0, 2).reshape(length, n_head * width)


def attention_forward(
    normed_q, normed_kv, qkv_w, out_w, down_pair, up_pair, seg_query, seg_key, causal
):
    n_head = lax.axis_size("head")
    piece_n, model_width = normed_q.shape
    heads_here = model_width // n_head // HEAD_DIM
    inner_q, lifted_q = adapter_forward(normed_q, down_pair[0], up_pair[0])
    inner_v, lifted_v = adapter_forward(normed_kv, down_pair[1], up_pair[1])
    queries = (contract(normed_q, qkv_w[0], 1, 0) + lifted_q).astype(jnp.bfloat16)
    keys = contract(normed_kv, qkv_w[1], 1, 0).astype(jnp.bfloat16)
    values = (contract(normed_kv, qkv_w[2], 1, 0) + lifted_v).astype(jnp.bfloat16)
    got = head_trade(
        jnp.stack([by_head(queries, n_head), by_head(keys, n_head), by_head(values, n_head)], 1)
    )
    queries_a, keys_a, values_a = [
        got[:, kind].reshape(n_head * piece_n, heads_here, HEAD_DIM) for kind in range(3)
    ]
    mixed_heads, row_tops, row_sums = attend_forward(
        queries_a, keys_a, values_a, seg_query, seg_key, causal
    )
    back_rows = from_head(head_trade(mixed_heads.reshape(n_head, piece_n, -1)))
    result = contract(back_rows, out_w, 1, 0)
    return (result, (inner_q, inner_v, queries_a, keys_a, values_a, row_tops, row_sums))


def attention_backward(
    grad_res,
    normed_q,
    normed_kv,
    kept_fwd,
    qkv_w,
    out_w,
    down_pair,
    up_pair,
    seg_query,
    seg_key,
    causal,
    want_inputs,
):
    inner_q, inner_v, queries_a, keys_a, values_a, row_tops, row_sums = kept_fwd
    n_head = lax.axis_size("head")
    head_at = lax.axis_index("head")
    piece_n, model_width = normed_q.shape
    group_w = model_width // n_head
    heads_here = group_w // HEAD_DIM
    grad_back = contract(grad_res.astype(jnp.bfloat16), out_w, 1, 1).astype(jnp.bfloat16)
    grad_mixed = head_trade(by_head(grad_back, n_head))
    grad_q, grad_k, grad_v = attend_backward(
        queries_a,
        keys_a,
        values_a,
        seg_query,
        seg_key,
        causal,
        row_tops,
        row_sums,
        grad_mixed.reshape(n_head * piece_n, heads_here, HEAD_DIM),
        want_inputs,
    )
    grad_q, grad_k, grad_v = [
        part.astype(jnp.bfloat16).reshape(n_head * piece_n, group_w)
        for part in (grad_q, grad_k, grad_v)
    ]
    if not want_inputs:
        inner_both = jnp.concatenate([inner_q, inner_v], axis=1).T
        inner_all = collected(inner_both, "head").transpose(1, 0, 2).reshape(
            2 * ADAPTER_RANK, n_head * piece_n
        )
        partial_inner = []
        up_gradients = []
        for at, grad_side in enumerate((grad_q, grad_v)):
            up_here = lax.dynamic_slice_in_dim(up_pair[at], head_at * group_w, group_w, 1)
            partial_inner.append(contract(up_here, grad_side, 1, 1))
            up_gradients.append(
                lax.dynamic_update_slice_in_dim(
                    jnp.zeros((ADAPTER_RANK, model_width), jnp.float32),
                    ADAPTER_SCALE
                    * contract(
                        inner_all[at * ADAPTER_RANK : (at + 1) * ADAPTER_RANK], grad_side, 1, 0
                    ),
                    head_at * group_w,
                    1,
                )
            )
        partial_inner = jnp.concatenate(partial_inner, axis=0)
        own_inner = scattered_sum(
            partial_inner.reshape(2 * ADAPTER_RANK, n_head, piece_n).transpose(1, 0, 2), "head"
        )
        own_inner = (ADAPTER_SCALE * own_inner).astype(jnp.bfloat16)
        return (
            None,
            None,
            (
                contract(own_inner[:ADAPTER_RANK], normed_q, 1, 0),
                contract(own_inner[ADAPTER_RANK:], normed_kv, 1, 0),
            ),
            tuple(up_gradients),
        )
    got = head_trade(
        jnp.stack([part.reshape(n_head, piece_n, group_w) for part in (grad_q, grad_k, grad_v)], 1)
    )
    grad_qt, grad_kt, grad_vt = [from_head(got[:, kind]) for kind in range(3)]
    down_query, up_query, side_q = adapter_back(
        grad_qt, inner_q, normed_q, down_pair[0], up_pair[0]
    )
    down_value, up_value, side_v = adapter_back(
        grad_vt, inner_v, normed_kv, down_pair[1], up_pair[1]
    )
    normed_query_gradient = contract(grad_qt, qkv_w[0], 1, 1) + side_q
    normed_key_value_gradient = (
        contract(grad_kt, qkv_w[1], 1, 1) + contract(grad_vt, qkv_w[2], 1, 1) + side_v
    )
    return (
        normed_query_gradient,
        normed_key_value_gradient,
        (down_query, down_value),
        (up_query, up_value),
    )


def whole_ffn(weight_pair):
    copies = lax.axis_size("dp") * lax.axis_size("head")
    copy_at = lax.axis_index("dp") * lax.axis_size("head") + lax.axis_index("head")
    units = weight_pair.shape[1] // copies
    share = lax.dynamic_slice_in_dim(weight_pair, copy_at * units, units, 1)
    share = jnp.concatenate([share[0], share[1]], axis=1)
    return lax.all_gather(share, ("dp", "head", "col"), axis=0, tiled=True)


def ffn_forward(normed_input, units):
    model_width = normed_input.shape[-1]
    pre_act = contract(normed_input, units[:, :model_width], 1, 1)
    hidden = jnp.maximum(pre_act, 0.0).astype(jnp.bfloat16)
    return (contract(hidden, units[:, model_width:], 1, 0), pre_act > 0.0)


def ffn_backward(grad_res, active, units):
    model_width = grad_res.shape[-1]
    grad_hidden = contract(grad_res.astype(jnp.bfloat16), units[:, model_width:], 1, 1)
    grad_pre = jnp.where(active, grad_hidden, 0.0).astype(jnp.bfloat16)
    return contract(grad_pre, units[:, :model_width], 1, 0)


def head_kernel(chunk, block, rows_ref, target_ref, table_ref, acc_ref, total_ref, base_ref, held, top_ref, sems):
    vocab_part = table_ref.shape[0]
    full = vocab_part // chunk
    tail = vocab_part - full * chunk
    tail_wide = -(-tail // 128) * 128
    blocks = rows_ref.shape[0] // block
    copies = [
        pltpu.make_async_copy(
            table_ref.at[pl.ds(at * chunk, size)], held.at[pl.ds(at * chunk, size)], sems.at[at]
        )
        for at, size in enumerate([chunk] * full + [tail] * (tail > 0))
    ]
    for copy in copies:
        copy.start()
    if tail_wide > tail:
        held[pl.ds(vocab_part, tail_wide - tail), :] = jnp.zeros(
            (tail_wide - tail, held.shape[1]), held.dtype
        )

    def dots(at, offset, width):
        return lax.dot_general(
            rows_ref[pl.ds(at * block, block), :],
            held[pl.ds(offset, width), :],
            (((1,), (1,)), ((), ())),
            preferred_element_type=jnp.float32,
        )

    def one_chunk(offset, width, used):
        table = held[pl.ds(offset, width), :]
        for at in range(blocks):
            rows_at = pl.ds(at * block, block)
            logits = dots(at, offset, width)
            places = lax.broadcasted_iota(jnp.int32, logits.shape, 1)
            if used < width:
                logits = jnp.where(places < used, logits, -1e30)
            weights = jnp.exp(logits - base_ref[rows_at, :])
            top_ref[rows_at, :] = jnp.maximum(
                top_ref[rows_at, :], jnp.max(logits, axis=1, keepdims=True)
            )
            total_ref[rows_at, :] += jnp.sum(weights, axis=1, keepdims=True)
            hit = places == target_ref[rows_at, :] - offset
            kept = jnp.where(hit, 0.0, weights).astype(jnp.bfloat16)
            acc_ref[rows_at, :] += jnp.dot(kept, table, preferred_element_type=jnp.float32)

    def one_pass(wait):
        acc_ref[...] = jnp.zeros_like(acc_ref)
        total_ref[...] = jnp.zeros_like(total_ref)

        def body(at, carry):
            if wait:
                pltpu.make_async_copy(
                    table_ref.at[pl.ds(0, chunk)], held.at[pl.ds(0, chunk)], sems.at[at]
                ).wait()
            one_chunk(pl.multiple_of(at * chunk, chunk), chunk, chunk)
            return carry

        lax.fori_loop(0, full, body, 0)
        if tail:
            if wait:
                copies[full].wait()
            one_chunk(full * chunk, tail_wide, tail)

    copies[0].wait()
    sample = min(256, chunk)
    for at in range(blocks):
        base_ref[pl.ds(at * block, block), :] = jnp.max(
            dots(at, 0, sample), axis=1, keepdims=True
        )
    top_ref[...] = base_ref[...]

    acc_ref[...] = jnp.zeros_like(acc_ref)
    total_ref[...] = jnp.zeros_like(total_ref)
    one_chunk(0, chunk, chunk)

    def body(at, carry):
        pltpu.make_async_copy(
            table_ref.at[pl.ds(0, chunk)], held.at[pl.ds(0, chunk)], sems.at[at]
        ).wait()
        one_chunk(pl.multiple_of(at * chunk, chunk), chunk, chunk)
        return carry

    lax.fori_loop(1, full, body, 0)
    if tail:
        copies[full].wait()
        one_chunk(full * chunk, tail_wide, tail)

    @pl.when(jnp.max(top_ref[...] - base_ref[...]) > 40.0)
    def _():
        base_ref[...] = top_ref[...]
        one_pass(False)


def head_pass(rows, targets, table, chunk=1024, block=256):
    tokens, width = rows.shape
    vocab_part = table.shape[0]
    full = vocab_part // chunk
    tail = vocab_part - full * chunk
    held_rows = full * chunk + -(-tail // 128) * 128
    column = jax.ShapeDtypeStruct((tokens, 1), jnp.float32)
    return pl.pallas_call(
        functools.partial(head_kernel, chunk, block),
        out_shape=(jax.ShapeDtypeStruct((tokens, width), jnp.float32), column, column),
        in_specs=[
            pl.BlockSpec(memory_space=pltpu.VMEM),
            pl.BlockSpec(memory_space=pltpu.VMEM),
            pl.BlockSpec(memory_space=pl.ANY),
        ],
        out_specs=tuple([pl.BlockSpec(memory_space=pltpu.VMEM)] * 3),
        scratch_shapes=[
            pltpu.VMEM((held_rows, width), table.dtype),
            pltpu.VMEM((tokens, 1), jnp.float32),
            pltpu.SemaphoreType.DMA((full + (tail > 0),)),
        ],
        compiler_params=pltpu.CompilerParams(vmem_limit_bytes=56 * 1024 * 1024),
    )(rows, targets, table)


def merge_stats(left_side, right_side):
    top_both = jnp.maximum(left_side[0], right_side[0])
    summed = left_side[1] * jnp.exp(left_side[0] - top_both) + right_side[1] * jnp.exp(
        right_side[0] - top_both
    )
    return (top_both, summed, left_side[2] + right_side[2])


def adam_update(weights, gradient, first_moment, second_moment, step_rate, step_count_float):
    first_new = BETA_ONE * first_moment + (1.0 - BETA_ONE) * gradient
    second_new = BETA_TWO * second_moment + (1.0 - BETA_TWO) * gradient * gradient
    first_hat = first_new / (1.0 - BETA_ONE**step_count_float)
    second_hat = second_new / (1.0 - BETA_TWO**step_count_float)
    weights_new = weights - step_rate * (
        first_hat / (jnp.sqrt(second_hat) + ADAM_EPS) + DECAY * weights
    )
    return (weights_new, first_new, second_new)


def per_device(
    encoder_token_ids,
    decoder_token_ids,
    target_token_ids,
    target_count_mask,
    encoder_document_length,
    decoder_document_length,
    embedding,
    attention_projection_weight,
    attention_output_weight,
    feedforward_weight,
    norm_gain_rows,
    earlier_down_weight,
    adapter_down_weight,
    adapter_up_weight,
    down_first_moment,
    down_second_moment,
    up_first_moment,
    up_second_moment,
    optimizer_step_count,
):
    n_col = lax.axis_size("col")
    col_at = lax.axis_index("col")
    vocab_part, model_width = embedding.shape
    tables = jnp.stack(
        [encoder_token_ids, decoder_token_ids, target_token_ids, target_count_mask]
    )
    tables = collected(tables, "col").transpose(1, 2, 0, 3)
    enc_all, dec_all, target_all, mask_all = tables.reshape(4, -1)

    def lookup(ids_flat):
        local_ids = ids_flat - col_at * vocab_part
        inside_ids = (local_ids >= 0) & (local_ids < vocab_part)
        picked = jnp.take(embedding, jnp.clip(local_ids, 0, vocab_part - 1), axis=0)
        return col_sums(
            jnp.where(inside_ids[:, None], picked, jnp.zeros((), picked.dtype))
        ).astype(jnp.float32)

    enc_state = lookup(enc_all)
    units_enc = whole_ffn(feedforward_weight[0])
    dec_state = lookup(dec_all)
    units_dec = whole_ffn(feedforward_weight[1])
    mask_float = mask_all.astype(jnp.float32)
    target_count = summed(jnp.sum(mask_float), ("dp", "head"))
    down_low_rank = adapter_down_weight.astype(jnp.bfloat16)
    up_low_rank = adapter_up_weight.astype(jnp.bfloat16)
    enc_seg = segment_of(
        lax.dynamic_index_in_dim(encoder_document_length, col_at, 0, keepdims=False), LEN
    )
    dec_seg = segment_of(
        lax.dynamic_index_in_dim(decoder_document_length, col_at, 0, keepdims=False), LEN
    )

    def weights_of(slot_at):
        return (
            attention_projection_weight[slot_at],
            attention_output_weight[slot_at],
            down_low_rank[2 * slot_at : 2 * slot_at + 2],
            up_low_rank[2 * slot_at : 2 * slot_at + 2],
        )

    enc_normed = rms_norm(enc_state, norm_gain_rows[0]).astype(jnp.bfloat16)
    branch_out, kept_enc = attention_forward(
        enc_normed, enc_normed, *weights_of(0), enc_seg, enc_seg, False
    )
    enc_mid = enc_state + branch_out
    dec_normed = rms_norm(dec_state, norm_gain_rows[3]).astype(jnp.bfloat16)
    branch_out, kept_self = attention_forward(
        dec_normed, dec_normed, *weights_of(1), dec_seg, dec_seg, True
    )
    dec_one = dec_state + branch_out
    branch_out, active_enc = ffn_forward(
        rms_norm(enc_mid, norm_gain_rows[1]).astype(jnp.bfloat16), units_enc
    )
    enc_last = enc_mid + branch_out
    encoded = rms_norm(enc_last, norm_gain_rows[2]).astype(jnp.bfloat16)
    cross_normed = rms_norm(dec_one, norm_gain_rows[4]).astype(jnp.bfloat16)
    branch_out, kept_cross = attention_forward(
        cross_normed, encoded, *weights_of(2), dec_seg, enc_seg, False
    )
    dec_two = dec_one + branch_out
    branch_out, active_dec = ffn_forward(
        rms_norm(dec_two, norm_gain_rows[5]).astype(jnp.bfloat16), units_dec
    )
    dec_three = dec_two + branch_out
    head_scale = MODEL_DIMENSION ** (-0.5)
    final_rows = (rms_norm(dec_three, norm_gain_rows[6]) * head_scale).astype(jnp.bfloat16)
    head_rows = col_rows(final_rows)
    local_t = target_all - col_at * vocab_part
    inside = (local_t >= 0) & (local_t < vocab_part)
    target_rows = jnp.take(
        embedding, jnp.clip(local_t, 0, vocab_part - 1), axis=0
    ).astype(jnp.float32)
    grad_rows, total_part, base_part = head_pass(head_rows, local_t[:, None], embedding)
    target_part = jnp.where(
        inside, jnp.sum(head_rows.astype(jnp.float32) * target_rows, axis=1), 0.0
    )
    base_part = base_part[:, 0]
    stats = (base_part, total_part[:, 0], target_part)
    step = 1
    while step < n_col:
        others = swapped(jnp.stack(stats), "col", step)
        stats = merge_stats(stats, (others[0], others[1], others[2]))
        step *= 2
    row_top, row_total, row_target = stats
    log_total = row_top + jnp.log(row_total)
    ce_total = summed(jnp.sum(mask_float * (log_total - row_target)), ("dp", "head"))
    coef = mask_float / target_count
    target_coef = (coef * (jnp.exp(target_part - log_total) - 1.0)).astype(jnp.bfloat16)
    target_coef = jnp.where(inside, target_coef.astype(jnp.float32), 0.0)
    grad_rows = (
        grad_rows * (coef * jnp.exp(base_part - log_total))[:, None]
        + target_coef[:, None] * target_rows
    )
    grad_final = col_sums(grad_rows.astype(jnp.bfloat16)).astype(jnp.float32)
    grad_dec = norm_back(dec_three, norm_gain_rows[6], grad_final, head_scale)
    grad_dec = grad_dec + norm_back(
        dec_two, norm_gain_rows[5], ffn_backward(grad_dec, active_dec, units_dec), 1.0
    )
    normed_query_gradient, grad_encoded, downs_cross, ups_cross = attention_backward(
        grad_dec, cross_normed, encoded, kept_cross, *weights_of(2), dec_seg, enc_seg, False, True
    )
    cross_sums = summed(jnp.stack(downs_cross + ups_cross), ("head", "dp", "col"))
    grad_dec = grad_dec + norm_back(dec_one, norm_gain_rows[4], normed_query_gradient, 1.0)
    unused_q, unused_kv, downs_self, ups_self = attention_backward(
        grad_dec, dec_normed, dec_normed, kept_self, *weights_of(1), dec_seg, dec_seg, True, False
    )
    grad_enc = norm_back(enc_last, norm_gain_rows[2], grad_encoded, 1.0)
    grad_enc = grad_enc + norm_back(
        enc_mid, norm_gain_rows[1], ffn_backward(grad_enc, active_enc, units_enc), 1.0
    )
    unused_q, unused_kv, downs_enc, ups_enc = attention_backward(
        grad_enc, enc_normed, enc_normed, kept_enc, *weights_of(0), enc_seg, enc_seg, False, False
    )
    self_sums = summed(
        jnp.stack(downs_enc + downs_self + ups_enc + ups_self), ("head", "dp", "col")
    )
    down_penalty_sum = jnp.concatenate([self_sums[:4], cross_sums[:2]])
    up_penalty_sum = jnp.concatenate([self_sums[4:], cross_sums[2:]])
    earlier_down_float = earlier_down_weight.astype(jnp.float32)
    intersection = jnp.einsum(
        "hygm,hvm->hygv", earlier_down_float, adapter_down_weight, precision=lax.Precision.HIGHEST
    )
    penalty = ORTH_WEIGHT * jnp.sum(intersection * intersection) + BASE_NORM_WEIGHT * jnp.sum(
        adapter_up_weight * adapter_up_weight
    )
    down_penalty_sum = down_penalty_sum + 2.0 * ORTH_WEIGHT * jnp.einsum(
        "aoij,aoid->ajd", intersection, earlier_down_float, precision=lax.Precision.HIGHEST
    )
    up_penalty_sum = up_penalty_sum + 2.0 * BASE_NORM_WEIGHT * adapter_up_weight
    loss_scalar = ce_total / target_count + penalty
    step_count_float = optimizer_step_count[0].astype(jnp.float32)
    updated_down_weight, down_first_updated, down_second_updated = adam_update(
        adapter_down_weight,
        down_penalty_sum,
        down_first_moment,
        down_second_moment,
        DOWN_STEP_RATE,
        step_count_float,
    )
    updated_up_weight, up_first_updated, up_second_updated = adam_update(
        adapter_up_weight,
        up_penalty_sum,
        up_first_moment,
        up_second_moment,
        UP_STEP_RATE,
        step_count_float,
    )
    return (
        loss_scalar,
        updated_down_weight,
        down_first_updated,
        down_second_updated,
        updated_up_weight,
        up_first_updated,
        up_second_updated,
    )


def solution(mesh):
    in_specs = (
        P("dp", ("head", "col")),
        P("dp", ("head", "col")),
        P("dp", ("head", "col")),
        P("dp", ("head", "col")),
        P("dp", None),
        P("dp", None),
        P("col", None),
        P(),
        P(),
        P(None, None, "col", None),
        P(),
        P(),
        P(),
        P(),
        P(),
        P(),
        P(),
        P(),
        P(),
    )
    out_specs = (P(), P(), P(), P(), P(), P(), P())
    return jax.shard_map(
        per_device, mesh=mesh, in_specs=in_specs, out_specs=out_specs, check_vma=False
    )
```
